256 devices in a mesh: row: 32 (over x, z_hi, y), col: 8 (over z_lo, core).
Axes of the slice: x: 4, y: 4, z: 8 (z_hi: 2, z_lo: 4; z = z_hi * 4 + z_lo), core: 2. Of those that a mesh axis runs over, the one named last changes fastest.
Arguments:
- green: bfloat16 [2, 2048, 16384], P(None, 'col', 'row'), may hold values from -6 to 6
- step_sigma: bfloat16 [2, 2048, 256], P(None, 'col'), may hold values from -0.21875 to 0.21875
- hist_sigma: bfloat16 [2, 4, 2048, 1024], P(None, None, 'col', 'row'), may hold values from -0.1875 to 0.1875
- green_hist: bfloat16 [2, 1792, 16384], P(None, None, 'row'), may hold values from -6 to 6
- resident: bfloat16 [2, 2048, 16384], P(None, 'col', 'row'), may hold values from -0.1875 to 0.1875
Outputs:
- green_out: bfloat16 [2, 2048, 16384], P(None, 'col', 'row')
- mirror_out: bfloat16 [2, 2048, 8192], P(None, 'col', 'row')
The draws below stay inside these ranges and needn't reach their ends.
All inputs are finite; a program needn't handle non-finite values.
Results may differ from the reference program's by a relative error of at most 0.014.
Values may be sent and summed in bfloat16 or wider, within the bound.
No kernel may reach another device: no remote copies, remote signals or barrier semaphores. Data moves between devices by JAX's collectives and lax.ppermute only.
A program may use at most 64 MiB of HBM per device.

```python
import jax
import jax.numpy as jnp

TB = 256
TPW = 512
HW = 4
TICKS = 4
HIST = 7
NT = 2048
NTP = 16384
N_ROW = 32
N_COL = 8


def shard_levels(key, shape, shards, low, largest):
    factor_of = 1.0
    for axis_at, blocks in shards:
        heights = jax.random.uniform(jax.random.fold_in(jax.random.fold_in(key, 6), axis_at), (blocks,), jnp.float32, low / len(shards), largest / len(shards))
        factor_of = factor_of * jnp.repeat(jnp.exp(heights), shape[axis_at] // blocks).reshape((-1,) + (1,) * (len(shape) - 1 - axis_at))
    return factor_of


def bell_draw(rng, dims, spread, most, split=(), dtype=jnp.bfloat16):
    array = jax.random.normal(rng, dims, jnp.float32) * spread
    if len(split) > 0:
        array = shard_levels(rng, dims, split, -0.22, 0.18) * array
    return jnp.clip(array, min=-most, max=most).astype(dtype)


def setup_inputs(seed: int = 0) -> dict:
    keys = jax.random.split(jax.random.key(seed), 6)
    return {
        "green": bell_draw(keys[0], (2, NT, NTP), 1.0, 6.0, ((1, 8), (2, 32))),
        "step_sigma": bell_draw(keys[1], (2, NT, TB), (3 * TB) ** -0.5, 0.21875, ((1, 8),)),
        "hist_sigma": bell_draw(keys[2], (2, TICKS, NT, HW * TB), (HW * TB) ** -0.5, 0.1875, ((2, 8), (3, 32))),
        "green_hist": bell_draw(keys[3], (2, HIST * TB, NTP), 1.0, 6.0, ((2, 32),)),
        "resident": bell_draw(keys[4], (2, NT, NTP), (2 * TPW) ** -0.5, 0.1875, ((1, 8), (2, 32))),
    }


time_step = 0.2


def complex_dot(left_real, left_imag, right_real, right_imag):
    real_part = jnp.dot(left_real, right_real, preferred_element_type=jnp.float32) - jnp.dot(left_imag, right_imag, preferred_element_type=jnp.float32)
    imag_part = jnp.dot(left_real, right_imag, preferred_element_type=jnp.float32) + jnp.dot(left_imag, right_real, preferred_element_type=jnp.float32)
    return real_part, imag_part


def advance(green_now, history, carried):
    real_part = green_now[0] + time_step * (history[1] + carried[1])
    imag_part = green_now[1] - time_step * (history[0] + carried[0])
    return jnp.stack([real_part, imag_part]).astype(jnp.bfloat16)


def reference(green, step_sigma, hist_sigma, green_hist, resident):
    histories = []
    for tick_index in range(TICKS):
        window = green_hist[:, tick_index * TB:(tick_index + HW) * TB]
        histories.append(complex_dot(hist_sigma[0, tick_index], hist_sigma[1, tick_index], window[0], window[1]))
    green_now = green
    for tick_index in range(TICKS):
        carried = jnp.zeros((2, TB, NTP), jnp.bfloat16)
        blocks = [carried]
        for block_index in range(N_COL - 1):
            row_span = slice(block_index * TB, (block_index + 1) * TB)
            real_part, imag_part = complex_dot(step_sigma[0, row_span], step_sigma[1, row_span], carried[0], carried[1])
            carried = jnp.stack([real_part + green_now[0, row_span], imag_part + green_now[1, row_span]]).astype(jnp.bfloat16)
            blocks.append(carried)
        carried_all = jnp.concatenate(blocks, axis=1)
        green_now = advance(green_now, histories[tick_index], carried_all)
    outputs = []
    for block_index in range(N_COL):
        row_span = slice(block_index * TB, (block_index + 1) * TB)
        mirrored = jnp.roll(green_now[:, row_span].reshape(2, TB, N_ROW, TPW), N_ROW // 2, axis=2).astype(jnp.float32)
        held = resident[:, row_span].reshape(2, TB, N_ROW, TPW).astype(jnp.float32)
        real_part = jnp.einsum("tra,sra->trs", held[0], mirrored[0]) + jnp.einsum("tra,sra->trs", held[1], mirrored[1])
        imag_part = jnp.einsum("tra,sra->trs", held[1], mirrored[0]) - jnp.einsum("tra,sra->trs", held[0], mirrored[1])
        outputs.append(jnp.stack([real_part, imag_part]).reshape(2, TB, N_ROW * TB))
    mirror_out = jnp.concatenate(outputs, axis=1).astype(jnp.bfloat16)
    return green_now, mirror_out
```

```python
import functools

import jax
import jax.numpy as jnp
from jax import lax
from jax.experimental import pallas as pl
from jax.experimental.pallas import tpu as pltpu
from jax.sharding import PartitionSpec as P

TB = 256
HW = 4
TICKS = 4
TIME_STEP = 0.2
BOTH = ("row", "col")
F32 = jnp.float32
BF16 = jnp.bfloat16


VMEM = pl.BlockSpec(memory_space=pltpu.VMEM)
SMEM = pl.BlockSpec(memory_space=pltpu.SMEM)


def pairs_of(move):
    pairs = []
    for row in range(32):
        for col in range(8):
            there = move(row // 8, (row // 4) % 2, row % 4, col // 2, col % 2)
            x, high, y, chip, core = there
            pairs.append((row * 8 + col, (x * 8 + high * 4 + y) * 8 + chip * 2 + core))
    return pairs


def send(value, move):
    return lax.ppermute(value, BOTH, pairs_of(move))


def first_mask(core):
    return 1 if core == 0 else 3


def second_mask(core):
    return 3 if core == 0 else 1


def x_first(x, high, y, chip, core):
    return x ^ first_mask(core), high, y, chip, core


def x_second(x, high, y, chip, core):
    return x ^ second_mask(core), high, y, chip, core


def y_first(x, high, y, chip, core):
    return x, high, y ^ first_mask(core), chip, core


def y_second(x, high, y, chip, core):
    return x, high, y ^ second_mask(core), chip, core


def other_high(x, high, y, chip, core):
    return x, high ^ 1, y, chip, core


def other_core(x, high, y, chip, core):
    return x, high, y, chip, core ^ 1


def other_branch(x, high, y, chip, core):
    return x ^ 2, high, y, chip, core


def next_chip(x, high, y, chip, core):
    along = (high * 4 + chip + 1) % 8
    return x, along // 4, y, along % 4, core


def call(kernel, outs, scratch, flops, moved, *args):
    specs = [SMEM] + [VMEM] * (len(args) - 1)
    return pl.pallas_call(
        kernel,
        out_shape=outs,
        in_specs=specs,
        out_specs=jax.tree.map(lambda _: VMEM, outs),
        scratch_shapes=scratch,
        compiler_params=pltpu.CompilerParams(vmem_limit_bytes=24 << 20),
        cost_estimate=pl.CostEstimate(flops=flops, bytes_accessed=moved, transcendentals=0),
    )(*args)


def dot(left, right):
    return jnp.dot(left, right, preferred_element_type=F32)


def complex_dot(left_real, left_imag, right_real, right_imag):
    real_part = dot(left_real, right_real) - dot(left_imag, right_imag)
    imag_part = dot(left_real, right_imag) + dot(left_imag, right_real)
    return real_part, imag_part


def shape(dims, dtype):
    return jax.ShapeDtypeStruct(dims, dtype)


def prepare_kernel(place_ref, sigma_ref, green_ref, swapped_ref, even_ref, odd_ref, both_ref, state_ref, base_ref):
    core = place_ref[4]
    first = core == 0
    own = green_ref[:, :, pl.ds(pl.multiple_of(core * TB, TB), TB)]
    even_ref[...] = jnp.where(first, sigma_ref[...], swapped_ref[0:2])
    odd_ref[...] = jnp.where(first, swapped_ref[0:2], sigma_ref[...])
    state_ref[0] = jnp.where(first, own, swapped_ref[2:4]).astype(F32)
    state_ref[1] = jnp.where(first, swapped_ref[2:4], own).astype(F32)
    real_part, imag_part = complex_dot(odd_ref[0], odd_ref[1], even_ref[0], even_ref[1])
    both_ref[0] = real_part.astype(BF16)
    both_ref[1] = imag_part.astype(BF16)
    set_base(odd_ref, state_ref, base_ref)


def set_base(odd_ref, state_ref, base_ref):
    real_part, imag_part = complex_dot(
        odd_ref[0], odd_ref[1], state_ref[0, 0].astype(BF16), state_ref[0, 1].astype(BF16)
    )
    base_ref[0] = real_part + state_ref[1, 0]
    base_ref[1] = imag_part + state_ref[1, 1]


def history_kernel(tick, place_ref, real_near_ref, real_far_ref, imag_near_ref, imag_far_ref, past_ref, keep_ref, give_ref, real_ref, imag_ref):
    x, high, y, core = place_ref[0], place_ref[1], place_ref[2], place_ref[4]
    first = jnp.where(core == 0, 1, 3)
    second = jnp.where(core == 0, 3, 1)
    masks = (0, first, second, 2)
    for outer in range(4):
        for inner in range(4):
            for deep in range(2):
                at_high = (high ^ deep) * 4
                real_at = ((x ^ masks[outer]) * 8 + at_high + (y ^ masks[inner])) * 32
                imag_at = ((x ^ masks[inner]) * 8 + at_high + (y ^ masks[outer])) * 32
                slot = (outer % 2) * 8 + inner * 2 + deep
                real_from = real_near_ref if outer < 2 else real_far_ref
                imag_from = imag_near_ref if outer < 2 else imag_far_ref
                real_ref[pl.ds(pl.multiple_of(real_at, 32), 32), :] = real_from[slot]
                imag_ref[pl.ds(pl.multiple_of(imag_at, 32), 32), :] = imag_from[slot]

    def turned(left, right):
        return lax.dot_general(left, right, (((0,), (0,)), ((), ())), preferred_element_type=F32)

    rows = slice(tick * TB, (tick + HW) * TB)
    for out_ref, side in ((give_ref, 1 - core), (keep_ref, core)):
        at = pl.ds(pl.multiple_of(side * TB, TB), TB)
        past_real = past_ref[0, rows, at]
        past_imag = past_ref[1, rows, at]
        out_ref[0] = (turned(real_ref[...], past_real) - turned(imag_ref[...], past_imag)).astype(BF16)
        out_ref[1] = (turned(real_ref[...], past_imag) + turned(imag_ref[...], past_real)).astype(BF16)


def first_link_kernel(place_ref, base_ref, out_ref):
    out_ref[...] = base_ref[...].astype(BF16)


def link_kernel(place_ref, both_ref, carry_ref, base_ref, out_ref):
    chip = place_ref[3]

    @pl.when(chip == 0)
    def _():
        out_ref[...] = base_ref[...].astype(BF16)

    @pl.when(chip > 0)
    def _():
        real_part, imag_part = complex_dot(both_ref[0], both_ref[1], carry_ref[0], carry_ref[1])
        out_ref[0] = (real_part + base_ref[0]).astype(BF16)
        out_ref[1] = (imag_part + base_ref[1]).astype(BF16)


def update_kernel(step, ticks, last, has_carry, place_ref, *refs):
    refs = list(refs)
    even_ref, odd_ref, state_ref, base_ref = refs[:4]
    refs = refs[4:]
    carry_ref = refs.pop(0) if has_carry else None
    pasts = [(refs.pop(0), refs.pop(0)) for _ in ticks]
    out_ref, other_ref, past_ref = refs
    chip, core = place_ref[3], place_ref[4]
    valid = (chip <= step) & (chip >= step - (TICKS - 1))

    def copy_past(keep_ref, swap_ref):
        first = core == 0
        past_ref[0] = jnp.where(first, keep_ref[...], swap_ref[...])
        past_ref[1] = jnp.where(first, swap_ref[...], keep_ref[...])

    @pl.when(valid)
    def _():
        for tick, (keep_ref, swap_ref) in zip(ticks, pasts):
            pl.when(chip == step - tick)(functools.partial(copy_past, keep_ref, swap_ref))
        state = [[state_ref[block, part] for part in range(2)] for block in range(2)]
        even_carry = [jnp.zeros((TB, TB), F32)] * 2
        odd_carry = state[0]
        if has_carry:
            inside = chip > 0
            carry = [jnp.where(inside, carry_ref[part], jnp.zeros((TB, TB), BF16)) for part in range(2)]
            even_carry = [part.astype(F32) for part in carry]
            moved = complex_dot(even_ref[0], even_ref[1], carry[0], carry[1])
            odd_carry = [moved[part] + state[0][part] for part in range(2)]
        carries = (even_carry, odd_carry)
        for block in range(2):
            past = [past_ref[block, part].astype(F32) for part in range(2)]
            new_real = state[block][0] + TIME_STEP * (past[1] + carries[block][1])
            new_imag = state[block][1] - TIME_STEP * (past[0] + carries[block][0])
            if last:
                past_ref[block, 0] = new_real.astype(BF16)
                past_ref[block, 1] = new_imag.astype(BF16)
            else:
                out_ref[block, 0] = new_real
                out_ref[block, 1] = new_imag
        if not last:
            set_base(odd_ref, out_ref, other_ref)

    @pl.when(jnp.logical_not(valid))
    def _():
        if last:
            past_ref[...] = state_ref[...].astype(BF16)
        else:
            out_ref[...] = state_ref[...]
            other_ref[...] = base_ref[...]

    if last:
        first = core == 0
        out_ref[...] = jnp.where(first, past_ref[0], past_ref[1])
        other_ref[...] = jnp.where(first, past_ref[1], past_ref[0])


def mirror_kernel(place_ref, resident_ref, keep_ref, swap_ref, out_ref):
    core = place_ref[4]

    def across(left, right):
        return lax.dot_general(left, right, (((1,), (1,)), ((), ())), preferred_element_type=F32)

    real_part = jnp.zeros((TB, TB), F32)
    imag_part = jnp.zeros((TB, TB), F32)
    for green_ref, side in ((keep_ref, core), (swap_ref, 1 - core)):
        at = pl.ds(pl.multiple_of(side * TB, TB), TB)
        held_real, held_imag = resident_ref[0, :, at], resident_ref[1, :, at]
        real_part += across(held_real, green_ref[0]) + across(held_imag, green_ref[1])
        imag_part += across(held_imag, green_ref[0]) - across(held_real, green_ref[1])
    out_ref[0] = real_part.astype(BF16)
    out_ref[1] = imag_part.astype(BF16)


def joined(near, far):
    return jnp.concatenate([near, far], axis=1)


def body(green, step_sigma, hist_sigma, green_hist, resident):
    row = lax.axis_index("row")
    col = lax.axis_index("col")
    core = col % 2
    place = jnp.stack([row // 8, (row // 4) % 2, row % 4, col // 2, core]).astype(jnp.int32)
    square = (2, TB, TB)
    unit = 8 * TB**3

    mine = jnp.swapaxes(hist_sigma, 2, 3)
    theirs = send(mine, other_high)
    real = jnp.stack([mine[0], theirs[0]], axis=1)
    imag = jnp.stack([mine[1], theirs[1]], axis=1)

    away = lax.dynamic_slice_in_dim(green, (1 - core) * TB, TB, axis=2)
    swapped = send(jnp.concatenate([step_sigma, away]), other_core)
    partner_resident = send(resident, other_branch)
    even, odd, both, state, base = call(
        prepare_kernel,
        (shape(square, BF16), shape(square, BF16), shape(square, BF16), shape((2, *square), F32), shape(square, F32)),
        [], 2 * unit, 4 << 20, place, step_sigma, green, swapped,
    )

    real = joined(real, send(real, y_first))
    imag = joined(imag, send(imag, x_first))
    real = joined(real, send(real, y_second))
    imag = joined(imag, send(imag, x_second))
    real_more = send(real, x_first)
    imag_more = send(imag, y_first)

    pasts = []
    for tick in range(TICKS):
        real_near = jnp.concatenate([real[tick], real_more[tick]])
        imag_near = jnp.concatenate([imag[tick], imag_more[tick]])
        real_far = send(real_near, x_second)
        imag_far = send(imag_near, y_second)
        keep, give = call(
            functools.partial(history_kernel, tick),
            (shape(square, BF16), shape(square, BF16)),
            [pltpu.VMEM((HW * TB, TB), BF16), pltpu.VMEM((HW * TB, TB), BF16)],
            8 * unit, 4 << 20, place, real_near, real_far, imag_near, imag_far, green_hist,
        )
        pasts.append((keep, send(give, other_core)))

    carry = None
    for step in range(7):
        last = step == 6
        if not last:
            if carry is None:
                link = call(first_link_kernel, shape(square, BF16), [], TB, 1 << 20, place, base)
            else:
                link = call(link_kernel, shape(square, BF16), [], unit, 1 << 20, place, both, carry, base)
        ticks = [step - chip for chip in range(4) if 0 <= step - chip < TICKS]
        args = [place, even, odd, state, base]
        if carry is not None:
            args.append(carry)
        for tick in ticks:
            args.extend(pasts[tick])
        outs = (shape(square, BF16), shape(square, BF16)) if last else (shape((2, *square), F32), shape(square, F32))
        new_carry = None if last else send(link, next_chip)
        state, base = call(
            functools.partial(update_kernel, step, ticks, last, carry is not None),
            outs, [pltpu.VMEM((2, *square), BF16)], 2 * unit, 4 << 20, *args,
        )
        carry = new_carry

    keep, give = state, base
    got = send(give, other_core)
    mirrored = call(mirror_kernel, shape(square, BF16), [], 2 * unit, 2 << 20, place, partner_resident, keep, got)
    mirror_out = send(mirrored, other_branch)
    green_out = jnp.where(core == 0, jnp.concatenate([keep, got], axis=2), jnp.concatenate([got, keep], axis=2))
    return green_out, mirror_out


def solution(mesh):
    placed = (
        P(None, "col", "row"),
        P(None, "col", None),
        P(None, None, "col", "row"),
        P(None, None, "row"),
        P(None, "col", "row"),
    )
    return jax.shard_map(
        body,
        mesh=mesh,
        in_specs=placed,
        out_specs=(P(None, "col", "row"), P(None, "col", "row")),
        check_vma=False,
    )
```

```python
import functools

import jax
import jax.numpy as jnp
from jax import lax
from jax.experimental import pallas as pl
from jax.experimental.pallas import tpu as pltpu
from jax.sharding import PartitionSpec as P


TB = 256
CHUNKS = 2
SHIFTS = (1, -1, 2)
OFFSETS = (0, -1, 1, 2)
BATCHES = ((0, 2), (2, 4))
PARTS = (((0, 1), (1, 2)), ((2, 4),))
WIDE = TB // CHUNKS
HW = 4
TICKS = 4
TIME_STEP = 0.2
BOTH = ("row", "col")
F32 = jnp.float32
BF16 = jnp.bfloat16


VMEM = pl.BlockSpec(memory_space=pltpu.VMEM)


def pairs_of(move):
    pairs = []
    for row in range(32):
        for col in range(8):
            there = move(row // 8, (row // 4) % 2, row % 4, col // 2, col % 2)
            if there is None:
                continue
            x, high, y, chip, core = there
            pairs.append((row * 8 + col, (x * 8 + high * 4 + y) * 8 + chip * 2 + core))
    return pairs


def send(value, move):
    return lax.ppermute(value, BOTH, pairs_of(move))


def early_axis(by):
    def move(x, high, y, chip, core):
        return (x, high, (y + by) % 4, chip, core) if core == 0 else ((x + by) % 4, high, y, chip, core)

    return move


def late_axis(by):
    def move(x, high, y, chip, core):
        return ((x + by) % 4, high, y, chip, core) if core == 0 else (x, high, (y + by) % 4, chip, core)

    return move


def other_high(x, high, y, chip, core):
    return x, high ^ 1, y, chip, core


def other_core(x, high, y, chip, core):
    return x, high, y, chip, core ^ 1


def other_branch(x, high, y, chip, core):
    return x ^ 2, high, y, chip, core


def next_chip(x, high, y, chip, core):
    return (x, high, y, chip + 1, core) if chip < 3 else None


def call(kernel, outs, scratch, flops, moved, *args):
    specs = [VMEM] * len(args)
    return pl.pallas_call(
        kernel,
        out_shape=outs,
        in_specs=specs,
        out_specs=jax.tree.map(lambda _: VMEM, outs),
        scratch_shapes=scratch,
        compiler_params=pltpu.CompilerParams(vmem_limit_bytes=24 << 20),
        cost_estimate=pl.CostEstimate(flops=flops, bytes_accessed=moved, transcendentals=0),
    )(*args)


def dot(left, right):
    return jnp.dot(left, right, preferred_element_type=F32)


def complex_dot(left_real, left_imag, right_real, right_imag):
    real_part = dot(left_real, right_real) - dot(left_imag, right_imag)
    imag_part = dot(left_real, right_imag) + dot(left_imag, right_real)
    return real_part, imag_part


def shape(dims, dtype):
    return jax.ShapeDtypeStruct(dims, dtype)


def place():
    row = lax.axis_index("row")
    col = lax.axis_index("col")
    return row // 8, (row // 4) % 2, row % 4, col // 2, col % 2


def load_kernel(mine_ref, out_ref):
    out_ref[...] = mine_ref[...]


def split_kernel(start, mine_ref, theirs_ref, out_ref):
    for at in range(out_ref.shape[0]):
        for part in range(2):
            out_ref[at, 0, part] = mine_ref[part, start + at]
            out_ref[at, 1, part] = theirs_ref[part, at]


def join_kernel(start, stop, *refs):
    out_ref = refs[-1]
    for slot, from_ref in enumerate(refs[:-1]):
        out_ref[slot] = from_ref[start:stop]


def pack_kernel(sigma_ref, green_ref, out_ref, own_ref):
    core = place()[4]
    out_ref[0:2] = sigma_ref[...]
    out_ref[2:4] = green_ref[:, :, pl.ds(pl.multiple_of((1 - core) * TB, TB), TB)]
    own_ref[...] = green_ref[:, :, pl.ds(pl.multiple_of(core * TB, TB), TB)]


def prepare_kernel(packed_ref, own_ref, swapped_ref, even_ref, odd_ref, both_ref, state_ref, base_ref, link_ref):
    core = place()[4]
    first = core == 0
    own = own_ref[...]
    even_ref[...] = jnp.where(first, packed_ref[0:2], swapped_ref[0:2])
    odd_ref[...] = jnp.where(first, swapped_ref[0:2], packed_ref[0:2])
    state_ref[0] = jnp.where(first, own, swapped_ref[2:4])
    state_ref[1] = jnp.where(first, swapped_ref[2:4], own)
    real_part, imag_part = complex_dot(odd_ref[0], odd_ref[1], even_ref[0], even_ref[1])
    both_ref[0] = real_part.astype(BF16)
    both_ref[1] = imag_part.astype(BF16)
    set_base(odd_ref, state_ref, base_ref)
    for half in range(CHUNKS):
        put_link(link_ref.at[half], base_ref, half)


def put_link(link_ref, base_ref, half):
    columns = slice(half * WIDE, (half + 1) * WIDE)
    link_ref[:, :WIDE] = base_ref[0, :, columns].astype(BF16)
    link_ref[:, WIDE:] = base_ref[1, :, columns].astype(BF16)


def set_base(odd_ref, state_ref, base_ref):
    real_part, imag_part = complex_dot(odd_ref[0], odd_ref[1], state_ref[0, 0], state_ref[0, 1])
    base_ref[0] = real_part + state_ref[1, 0].astype(F32)
    base_ref[1] = imag_part + state_ref[1, 1].astype(F32)


def history_kernel(tick, stacked, *refs):
    sigma_refs = refs[:4]
    past_ref, keep_ref, give_ref, real_ref, imag_ref = refs[4:]
    x, high, y, _, core = place()
    upright = core == 0
    for outer in range(4):
        for inner in range(4):
            x_at = (x + jnp.where(upright, OFFSETS[outer], OFFSETS[inner]) + 4) % 4
            y_at = (y + jnp.where(upright, OFFSETS[inner], OFFSETS[outer]) + 4) % 4
            for deep in range(2):
                at = pl.ds(pl.multiple_of((x_at * 8 + (high ^ deep) * 4 + y_at) * 32, 32), 32)
                real_ref[at, :] = sigma_refs[outer][inner, stacked, deep, 0]
                imag_ref[at, :] = sigma_refs[outer][inner, stacked, deep, 1]

    def turned(left, right):
        return lax.dot_general(left, right, (((0,), (0,)), ((), ())), preferred_element_type=F32)

    rows = slice(tick * TB, (tick + HW) * TB)
    for out_ref, side in ((give_ref, 1 - core), (keep_ref, core)):
        at = pl.ds(pl.multiple_of(side * TB, TB), TB)
        past_real = past_ref[0, rows, at]
        past_imag = past_ref[1, rows, at]
        out_ref[0] = (turned(real_ref[...], past_real) - turned(imag_ref[...], past_imag)).astype(BF16)
        out_ref[1] = (turned(real_ref[...], past_imag) + turned(imag_ref[...], past_real)).astype(BF16)


def link_kernel(half, early, both_ref, carry_ref, base_ref, out_ref):
    chip = place()[3]

    @pl.when(chip == 0)
    def _():
        put_link(out_ref, base_ref, half)

    @pl.when(chip > 0)
    def _():
        carry = carry_ref[half] if early else carry_ref[...]
        columns = slice(half * WIDE, (half + 1) * WIDE)
        by_real = dot(both_ref[0], carry)
        by_imag = dot(both_ref[1], carry)
        out_ref[:, :WIDE] = (by_real[:, :WIDE] - by_imag[:, WIDE:] + base_ref[0, :, columns]).astype(BF16)
        out_ref[:, WIDE:] = (by_real[:, WIDE:] + by_imag[:, :WIDE] + base_ref[1, :, columns]).astype(BF16)


def update_kernel(step, ticks, n_carry, *refs):
    refs = list(refs)
    last = step == 6
    even_ref, odd_ref, state_ref, base_ref = refs[:4]
    carry_refs = refs[4 : 4 + n_carry]
    refs = refs[4 + n_carry :]
    pasts = [(refs.pop(0), refs.pop(0)) for _ in ticks]
    out_ref, other_ref, past_ref = refs
    _, _, _, chip, core = place()
    valid = (chip <= step) & (chip >= step - (TICKS - 1))

    def copy_past(keep_ref, swap_ref):
        first = core == 0
        past_ref[0] = jnp.where(first, keep_ref[...], swap_ref[...])
        past_ref[1] = jnp.where(first, swap_ref[...], keep_ref[...])

    @pl.when(valid)
    def _():
        for tick, (keep_ref, swap_ref) in zip(ticks, pasts):
            pl.when(chip == step - tick)(functools.partial(copy_past, keep_ref, swap_ref))
        state = [[state_ref[block, part].astype(F32) for part in range(2)] for block in range(2)]
        even_carry = [jnp.zeros((TB, TB), F32)] * 2
        odd_carry = state[0]
        if n_carry:
            inside = chip > 0
            halves = [carry_refs[0][half] for half in range(CHUNKS)] if step == 1 else [ref[...] for ref in carry_refs]
            carry = [
                jnp.concatenate([half[:, part * WIDE : (part + 1) * WIDE] for half in halves], axis=1)
                for part in range(2)
            ]
            carry = [jnp.where(inside, part, jnp.zeros((TB, TB), BF16)) for part in carry]
            even_carry = [part.astype(F32) for part in carry]
            moved = complex_dot(even_ref[0], even_ref[1], carry[0], carry[1])
            odd_carry = [moved[part] + state[0][part] for part in range(2)]
        carries = (even_carry, odd_carry)
        new_ref = past_ref if last else out_ref
        for block in range(2):
            past = [past_ref[block, part].astype(F32) for part in range(2)]
            new_real = state[block][0] + TIME_STEP * (past[1] + carries[block][1])
            new_imag = state[block][1] - TIME_STEP * (past[0] + carries[block][0])
            new_ref[block, 0] = new_real.astype(BF16)
            new_ref[block, 1] = new_imag.astype(BF16)
        if not last:
            set_base(odd_ref, out_ref, other_ref)

    @pl.when(jnp.logical_not(valid))
    def _():
        if last:
            past_ref[...] = state_ref[...]
        else:
            out_ref[...] = state_ref[...]
            other_ref[...] = base_ref[...]

    if last:
        first = core == 0
        out_ref[...] = jnp.where(first, past_ref[0], past_ref[1])
        other_ref[...] = jnp.where(first, past_ref[1], past_ref[0])


def mirror_kernel(resident_ref, keep_ref, swap_ref, out_ref):
    core = place()[4]

    def across(left, right):
        return lax.dot_general(left, right, (((1,), (1,)), ((), ())), preferred_element_type=F32)

    real_part = jnp.zeros((TB, TB), F32)
    imag_part = jnp.zeros((TB, TB), F32)
    for green_ref, side in ((keep_ref, core), (swap_ref, 1 - core)):
        at = pl.ds(pl.multiple_of(side * TB, TB), TB)
        held_real, held_imag = resident_ref[0, :, at], resident_ref[1, :, at]
        real_part += across(held_real, green_ref[0]) + across(held_imag, green_ref[1])
        imag_part += across(held_imag, green_ref[0]) - across(held_real, green_ref[1])
    out_ref[0] = real_part.astype(BF16)
    out_ref[1] = imag_part.astype(BF16)


def steps(green, step_sigma, hist_sigma, green_hist, resident):
    core = lax.axis_index("col") % 2
    square = (2, TB, TB)
    unit = 8 * TB**3
    pair = (shape(square, BF16), shape(square, BF16))
    state_shape = (shape((2, *square), BF16), shape(square, F32))

    mine = jnp.swapaxes(hist_sigma, 2, 3)
    theirs = [send(mine[:, start:stop], other_high) for start, stop in BATCHES]
    loaded = call(load_kernel, shape(mine.shape, BF16), [], TB, 1 << 18, mine)

    packed, own_green = call(
        pack_kernel, (shape((4, TB, TB), BF16), shape(square, BF16)), [], TB, 1 << 20, step_sigma, green
    )
    swapped = send(packed, other_core)
    partner_resident = send(resident, other_branch)
    even, odd, both, state, base, link = call(
        prepare_kernel, (shape(square, BF16), *pair, *state_shape, shape((CHUNKS, TB, 2 * WIDE), BF16)),
        [], 2 * unit, 4 << 20, packed, own_green, swapped,
    )
    carries = [send(link, next_chip)]

    pasts = []
    for batch, (start, stop) in enumerate(BATCHES):
        own = call(
            functools.partial(split_kernel, start),
            shape((stop - start, 2, 2, 32, TB), BF16), [], TB, 1 << 19, loaded, theirs[batch],
        )
        near = [own] + [send(own, early_axis(by)) for by in SHIFTS]
        for first, end in PARTS[batch]:
            block = call(
                functools.partial(join_kernel, first - start, end - start),
                shape((4, end - first, 2, 2, 32, TB), BF16), [], TB, 1 << 20, *near,
            )
            far = [send(block, late_axis(by)) for by in SHIFTS]
            for tick in range(first, end):
                keep, give = call(
                    functools.partial(history_kernel, tick, tick - first),
                    pair, [pltpu.VMEM((HW * TB, TB), BF16), pltpu.VMEM((HW * TB, TB), BF16)],
                    8 * unit, 4 << 20, block, *far, green_hist,
                )
                pasts.append((keep, send(give, other_core)))

    for step in range(7):
        new_carries = carries
        if 0 < step < 6:
            new_carries = []
            for half in range(CHUNKS):
                early = step == 1
                link = call(
                    functools.partial(link_kernel, half, early),
                    shape((TB, 2 * WIDE), BF16), [], unit, 1 << 19, both, carries[0 if early else half], base,
                )
                new_carries.append(send(link, next_chip))
        ticks = [step - chip for chip in range(4) if 0 <= step - chip < TICKS]
        used = carries if step else []
        args = [even, odd, state, base, *used]
        for tick in ticks:
            args.extend(pasts[tick])
        state, base = call(
            functools.partial(update_kernel, step, ticks, len(used)),
            pair if step == 6 else state_shape, [pltpu.VMEM((2, *square), BF16)], 2 * unit, 4 << 20, *args,
        )
        carries = new_carries

    keep, give = state, base
    got = send(give, other_core)
    mirrored = call(mirror_kernel, shape(square, BF16), [], 2 * unit, 2 << 20, partner_resident, keep, got)
    mirror_out = send(mirrored, other_branch)
    green_out = jnp.where(core == 0, jnp.concatenate([keep, got], axis=2), jnp.concatenate([got, keep], axis=2))
    return green_out, mirror_out


def solution(mesh):
    placed = (
        P(None, "col", "row"),
        P(None, "col", None),
        P(None, None, "col", "row"),
        P(None, None, "row"),
        P(None, "col", "row"),
    )
    return jax.shard_map(
        steps,
        mesh=mesh,
        in_specs=placed,
        out_specs=(P(None, "col", "row"), P(None, "col", "row")),
        check_vma=False,
    )
```

```python
import functools

import jax
import jax.numpy as jnp
from jax import lax
from jax.experimental import pallas as pl
from jax.experimental.pallas import tpu as pltpu
from jax.sharding import PartitionSpec as P


TB = 256
CHUNKS = 2
SHIFTS = (1, -1, 2)
OFFSETS = (0, -1, 1, 2)
BATCHES = ((0, 2), (2, 4))
PARTS = (((0, 1), (1, 2)), ((2, 4),))
WIDE = TB // CHUNKS
HW = 4
TICKS = 4
TIME_STEP = 0.2
BOTH = ("row", "col")
F32 = jnp.float32
BF16 = jnp.bfloat16


VMEM = pl.BlockSpec(memory_space=pltpu.VMEM)


def pairs_of(move):
    pairs = []
    for row in range(32):
        for col in range(8):
            there = move(row // 8, (row // 4) % 2, row % 4, col // 2, col % 2)
            x, high, y, chip, core = there
            pairs.append((row * 8 + col, (x * 8 + high * 4 + y) * 8 + chip * 2 + core))
    return pairs


def send(value, move):
    return lax.ppermute(value, BOTH, pairs_of(move))


def early_axis(by):
    def move(x, high, y, chip, core):
        return (x, high, (y + by) % 4, chip, core) if core == 0 else ((x + by) % 4, high, y, chip, core)

    return move


def late_axis(by):
    def move(x, high, y, chip, core):
        return ((x + by) % 4, high, y, chip, core) if core == 0 else (x, high, (y + by) % 4, chip, core)

    return move


def other_high(x, high, y, chip, core):
    return x, high ^ 1, y, chip, core


def other_core(x, high, y, chip, core):
    return x, high, y, chip, core ^ 1


def other_branch(x, high, y, chip, core):
    return x ^ 2, high, y, chip, core


def next_chip(step):
    first = max(step - (TICKS - 1), 0)
    last = min(step, 2) + 1

    def move(x, high, y, chip, core):
        if first <= chip < last:
            return x, high, y, chip + 1, core
        if chip == last:
            return x, high, y, first, core
        return x, high, y, chip, core ^ 1

    return move


def call(kernel, outs, scratch, flops, moved, *args):
    specs = [VMEM] * len(args)
    return pl.pallas_call(
        kernel,
        out_shape=outs,
        in_specs=specs,
        out_specs=jax.tree.map(lambda _: VMEM, outs),
        scratch_shapes=scratch,
        compiler_params=pltpu.CompilerParams(vmem_limit_bytes=24 << 20),
        cost_estimate=pl.CostEstimate(flops=flops, bytes_accessed=moved, transcendentals=0),
    )(*args)


def dot(left, right):
    return jnp.dot(left, right, preferred_element_type=F32)


def complex_dot(left_real, left_imag, right_real, right_imag):
    real_part = dot(left_real, right_real) - dot(left_imag, right_imag)
    imag_part = dot(left_real, right_imag) + dot(left_imag, right_real)
    return real_part, imag_part


def shape(dims, dtype):
    return jax.ShapeDtypeStruct(dims, dtype)


def place():
    row = lax.axis_index("row")
    col = lax.axis_index("col")
    return row // 8, (row // 4) % 2, row % 4, col // 2, col % 2


def load_kernel(mine_ref, out_ref):
    out_ref[...] = mine_ref[...]


def split_kernel(start, mine_ref, theirs_ref, out_ref):
    for at in range(out_ref.shape[0]):
        for part in range(2):
            out_ref[at, 0, part] = mine_ref[part, start + at]
            out_ref[at, 1, part] = theirs_ref[part, at]


def join_kernel(start, stop, *refs):
    out_ref = refs[-1]
    for slot, from_ref in enumerate(refs[:-1]):
        out_ref[slot] = from_ref[start:stop]


def pack_kernel(sigma_ref, green_ref, out_ref, own_ref):
    core = place()[4]
    out_ref[0:2] = sigma_ref[...]
    out_ref[2:4] = green_ref[:, :, pl.ds(pl.multiple_of((1 - core) * TB, TB), TB)]
    own_ref[...] = green_ref[:, :, pl.ds(pl.multiple_of(core * TB, TB), TB)]


def prepare_kernel(packed_ref, own_ref, swapped_ref, even_ref, odd_ref, both_ref, state_ref, base_ref, link_ref):
    core = place()[4]
    first = core == 0
    own = own_ref[...]
    even_ref[...] = jnp.where(first, packed_ref[0:2], swapped_ref[0:2])
    odd_ref[...] = jnp.where(first, swapped_ref[0:2], packed_ref[0:2])
    state_ref[0] = jnp.where(first, own, swapped_ref[2:4])
    state_ref[1] = jnp.where(first, swapped_ref[2:4], own)
    real_part, imag_part = complex_dot(odd_ref[0], odd_ref[1], even_ref[0], even_ref[1])
    both_ref[0] = real_part.astype(BF16)
    both_ref[1] = imag_part.astype(BF16)
    set_base(odd_ref, state_ref, base_ref)
    for half in range(CHUNKS):
        put_link(link_ref.at[half], base_ref, half)


def put_link(link_ref, base_ref, half):
    columns = slice(half * WIDE, (half + 1) * WIDE)
    link_ref[:, :WIDE] = base_ref[0, :, columns].astype(BF16)
    link_ref[:, WIDE:] = base_ref[1, :, columns].astype(BF16)


def set_base(odd_ref, state_ref, base_ref):
    real_part, imag_part = complex_dot(odd_ref[0], odd_ref[1], state_ref[0, 0], state_ref[0, 1])
    base_ref[0] = real_part + state_ref[1, 0].astype(F32)
    base_ref[1] = imag_part + state_ref[1, 1].astype(F32)


def turned(left, right):
    return lax.dot_general(left, right, (((0,), (0,)), ((), ())), preferred_element_type=F32)


def put_history(tick, side, real_ref, imag_ref, past_ref, out_ref):
    rows = slice(tick * TB, (tick + HW) * TB)
    at = pl.ds(pl.multiple_of(side * TB, TB), TB)
    past_real = past_ref[0, rows, at]
    past_imag = past_ref[1, rows, at]
    out_ref[0] = (turned(real_ref[...], past_real) - turned(imag_ref[...], past_imag)).astype(BF16)
    out_ref[1] = (turned(real_ref[...], past_imag) + turned(imag_ref[...], past_real)).astype(BF16)


def keep_kernel(tick, real_ref, imag_ref, past_ref, out_ref):
    put_history(tick, place()[4], real_ref, imag_ref, past_ref, out_ref)


def history_kernel(tick, stacked, *refs):
    sigma_refs = refs[:4]
    past_ref, give_ref, real_ref, imag_ref = refs[4:]
    x, high, y, _, core = place()
    upright = core == 0
    for outer in range(4):
        for inner in range(4):
            x_at = (x + jnp.where(upright, OFFSETS[outer], OFFSETS[inner]) + 4) % 4
            y_at = (y + jnp.where(upright, OFFSETS[inner], OFFSETS[outer]) + 4) % 4
            for deep in range(2):
                at = pl.ds(pl.multiple_of((x_at * 8 + (high ^ deep) * 4 + y_at) * 32, 32), 32)
                real_ref[at, :] = sigma_refs[outer][inner, stacked, deep, 0]
                imag_ref[at, :] = sigma_refs[outer][inner, stacked, deep, 1]

    put_history(tick, 1 - core, real_ref, imag_ref, past_ref, give_ref)


def link_kernel(half, early, both_ref, carry_ref, base_ref, out_ref):
    chip = place()[3]

    @pl.when(chip == 0)
    def _():
        put_link(out_ref, base_ref, half)

    @pl.when(chip > 0)
    def _():
        carry = carry_ref[half] if early else carry_ref[...]
        columns = slice(half * WIDE, (half + 1) * WIDE)
        by_real = dot(both_ref[0], carry)
        by_imag = dot(both_ref[1], carry)
        out_ref[:, :WIDE] = (by_real[:, :WIDE] - by_imag[:, WIDE:] + base_ref[0, :, columns]).astype(BF16)
        out_ref[:, WIDE:] = (by_real[:, WIDE:] + by_imag[:, :WIDE] + base_ref[1, :, columns]).astype(BF16)


def update_kernel(step, ticks, n_carry, *refs):
    refs = list(refs)
    last = step == 6
    even_ref, odd_ref, state_ref, base_ref = refs[:4]
    carry_refs = refs[4 : 4 + n_carry]
    refs = refs[4 + n_carry :]
    pasts = [(refs.pop(0), refs.pop(0)) for _ in ticks]
    out_ref, other_ref, past_ref = refs
    _, _, _, chip, core = place()
    valid = (chip <= step) & (chip >= step - (TICKS - 1))

    def copy_past(keep_ref, swap_ref):
        first = core == 0
        past_ref[0] = jnp.where(first, keep_ref[...], swap_ref[...])
        past_ref[1] = jnp.where(first, swap_ref[...], keep_ref[...])

    @pl.when(valid)
    def _():
        for tick, (keep_ref, swap_ref) in zip(ticks, pasts):
            pl.when(chip == step - tick)(functools.partial(copy_past, keep_ref, swap_ref))
        state = [[state_ref[block, part].astype(F32) for part in range(2)] for block in range(2)]
        even_carry = [jnp.zeros((TB, TB), F32)] * 2
        odd_carry = state[0]
        if n_carry:
            inside = chip > 0
            halves = [carry_refs[0][half] for half in range(CHUNKS)] if step == 1 else [ref[...] for ref in carry_refs]
            carry = [
                jnp.concatenate([half[:, part * WIDE : (part + 1) * WIDE] for half in halves], axis=1)
                for part in range(2)
            ]
            carry = [jnp.where(inside, part, jnp.zeros((TB, TB), BF16)) for part in carry]
            even_carry = [part.astype(F32) for part in carry]
            moved = complex_dot(even_ref[0], even_ref[1], carry[0], carry[1])
            odd_carry = [moved[part] + state[0][part] for part in range(2)]
        carries = (even_carry, odd_carry)
        new_ref = past_ref if last else out_ref
        for block in range(2):
            past = [past_ref[block, part].astype(F32) for part in range(2)]
            new_real = state[block][0] + TIME_STEP * (past[1] + carries[block][1])
            new_imag = state[block][1] - TIME_STEP * (past[0] + carries[block][0])
            new_ref[block, 0] = new_real.astype(BF16)
            new_ref[block, 1] = new_imag.astype(BF16)
        if not last:
            set_base(odd_ref, out_ref, other_ref)

    @pl.when(jnp.logical_not(valid))
    def _():
        if last:
            past_ref[...] = state_ref[...]
        else:
            out_ref[...] = state_ref[...]
            other_ref[...] = base_ref[...]

    if last:
        first = core == 0
        out_ref[...] = jnp.where(first, past_ref[0], past_ref[1])
        other_ref[...] = jnp.where(first, past_ref[1], past_ref[0])


def mirror_kernel(resident_ref, keep_ref, swap_ref, out_ref):
    core = place()[4]

    def across(left, right):
        return lax.dot_general(left, right, (((1,), (1,)), ((), ())), preferred_element_type=F32)

    real_part = jnp.zeros((TB, TB), F32)
    imag_part = jnp.zeros((TB, TB), F32)
    for green_ref, side in ((keep_ref, core), (swap_ref, 1 - core)):
        at = pl.ds(pl.multiple_of(side * TB, TB), TB)
        held_real, held_imag = resident_ref[0, :, at], resident_ref[1, :, at]
        real_part += across(held_real, green_ref[0]) + across(held_imag, green_ref[1])
        imag_part += across(held_imag, green_ref[0]) - across(held_real, green_ref[1])
    out_ref[0] = real_part.astype(BF16)
    out_ref[1] = imag_part.astype(BF16)


def steps(green, step_sigma, hist_sigma, green_hist, resident):
    core = lax.axis_index("col") % 2
    square = (2, TB, TB)
    unit = 8 * TB**3
    pair = (shape(square, BF16), shape(square, BF16))
    state_shape = (shape((2, *square), BF16), shape(square, F32))

    mine = jnp.swapaxes(hist_sigma, 2, 3)
    theirs = [send(mine[:, start:stop], other_high) for start, stop in BATCHES]
    loaded = call(load_kernel, shape(mine.shape, BF16), [], TB, 1 << 18, mine)

    packed, own_green = call(
        pack_kernel, (shape((4, TB, TB), BF16), shape(square, BF16)), [], TB, 1 << 20, step_sigma, green
    )
    swapped = send(packed, other_core)
    partner_resident = send(resident, other_branch)
    even, odd, both, state, base, link = call(
        prepare_kernel, (shape(square, BF16), *pair, *state_shape, shape((CHUNKS, TB, 2 * WIDE), BF16)),
        [], 2 * unit, 4 << 20, packed, own_green, swapped,
    )
    carries = [send(link, next_chip(0))]

    pasts = []
    for batch, (start, stop) in enumerate(BATCHES):
        own = call(
            functools.partial(split_kernel, start),
            shape((stop - start, 2, 2, 32, TB), BF16), [], TB, 1 << 19, loaded, theirs[batch],
        )
        near = [own] + [send(own, early_axis(by)) for by in SHIFTS]
        for first, end in PARTS[batch]:
            block = call(
                functools.partial(join_kernel, first - start, end - start),
                shape((4, end - first, 2, 2, 32, TB), BF16), [], TB, 1 << 20, *near,
            )
            far = [send(block, late_axis(by)) for by in SHIFTS]
            for tick in range(first, end):
                table = shape((HW * TB, TB), BF16)
                give, real, imag = call(
                    functools.partial(history_kernel, tick, tick - first),
                    (shape(square, BF16), table, table), [], 4 * unit, 4 << 20, block, *far, green_hist,
                )
                traded = send(give, other_core)
                keep = call(
                    functools.partial(keep_kernel, tick),
                    shape(square, BF16), [], 4 * unit, 3 << 20, real, imag, green_hist,
                )
                pasts.append((keep, traded))

    for step in range(7):
        new_carries = carries
        if 0 < step < 6:
            new_carries = []
            for half in range(CHUNKS):
                early = step == 1
                link = call(
                    functools.partial(link_kernel, half, early),
                    shape((TB, 2 * WIDE), BF16), [], unit, 1 << 19, both, carries[0 if early else half], base,
                )
                new_carries.append(send(link, next_chip(step)))
        ticks = [step - chip for chip in range(4) if 0 <= step - chip < TICKS]
        used = carries if step else []
        args = [even, odd, state, base, *used]
        for tick in ticks:
            args.extend(pasts[tick])
        state, base = call(
            functools.partial(update_kernel, step, ticks, len(used)),
            pair if step == 6 else state_shape, [pltpu.VMEM((2, *square), BF16)], 2 * unit, 4 << 20, *args,
        )
        carries = new_carries

    keep, give = state, base
    got = send(give, other_core)
    mirrored = call(mirror_kernel, shape(square, BF16), [], 2 * unit, 2 << 20, partner_resident, keep, got)
    mirror_out = send(mirrored, other_branch)
    green_out = jnp.where(core == 0, jnp.concatenate([keep, got], axis=2), jnp.concatenate([got, keep], axis=2))
    return green_out, mirror_out


def solution(mesh):
    placed = (
        P(None, "col", "row"),
        P(None, "col", None),
        P(None, None, "col", "row"),
        P(None, None, "row"),
        P(None, "col", "row"),
    )
    return jax.shard_map(
        steps,
        mesh=mesh,
        in_specs=placed,
        out_specs=(P(None, "col", "row"), P(None, "col", "row")),
        check_vma=False,
    )
```

```python
import functools

import jax
import jax.numpy as jnp
from jax import lax
from jax.experimental import pallas as pl
from jax.experimental.pallas import tpu as pltpu
from jax.sharding import PartitionSpec as P


TB = 256
CHUNKS = 2
SHIFTS = (1, -1, 2)
OFFSETS = (0, -1, 1, 2)
BATCHES = ((0, 2), (2, 4))
PARTS = (((0, 1), (1, 2)), ((2, 4),))
WIDE = TB // CHUNKS
HW = 4
TICKS = 4
TIME_STEP = 0.2
BOTH = ("row", "col")
F32 = jnp.float32
BF16 = jnp.bfloat16


VMEM = pl.BlockSpec(memory_space=pltpu.VMEM)


def pairs_of(move):
    pairs = []
    for row in range(32):
        for col in range(8):
            there = move(row // 8, (row // 4) % 2, row % 4, col // 2, col % 2)
            x, high, y, chip, core = there
            pairs.append((row * 8 + col, (x * 8 + high * 4 + y) * 8 + chip * 2 + core))
    return pairs


def send(value, move):
    return lax.ppermute(value, BOTH, pairs_of(move))


def early_axis(by):
    def move(x, high, y, chip, core):
        return (x, high, (y + by) % 4, chip, core) if core == 0 else ((x + by) % 4, high, y, chip, core)

    return move


def late_axis(by):
    def move(x, high, y, chip, core):
        return ((x + by) % 4, high, y, chip, core) if core == 0 else (x, high, (y + by) % 4, chip, core)

    return move


def other_high(x, high, y, chip, core):
    return x, high ^ 1, y, chip, core


def other_core(x, high, y, chip, core):
    return x, high, y, chip, core ^ 1


def other_branch(x, high, y, chip, core):
    return x ^ 2, high, y, chip, core


def next_chip(step):
    first = max(step - (TICKS - 1), 0)
    last = min(step, 2) + 1

    def move(x, high, y, chip, core):
        if first <= chip < last:
            return x, high, y, chip + 1, core
        if chip == last:
            return x, high, y, first, core
        return x, high, y, chip, core ^ 1

    return move


def call(kernel, outs, scratch, flops, moved, *args):
    specs = [VMEM] * len(args)
    return pl.pallas_call(
        kernel,
        out_shape=outs,
        in_specs=specs,
        out_specs=jax.tree.map(lambda _: VMEM, outs),
        scratch_shapes=scratch,
        compiler_params=pltpu.CompilerParams(vmem_limit_bytes=24 << 20),
        cost_estimate=pl.CostEstimate(flops=flops, bytes_accessed=moved, transcendentals=0),
    )(*args)


def dot(left, right):
    return jnp.dot(left, right, preferred_element_type=F32)


def complex_dot(left_real, left_imag, right_real, right_imag):
    real_part = dot(left_real, right_real) - dot(left_imag, right_imag)
    imag_part = dot(left_real, right_imag) + dot(left_imag, right_real)
    return real_part, imag_part


def shape(dims, dtype):
    return jax.ShapeDtypeStruct(dims, dtype)


def place():
    row = lax.axis_index("row")
    col = lax.axis_index("col")
    return row // 8, (row // 4) % 2, row % 4, col // 2, col % 2


def load_kernel(mine_ref, out_ref):
    out_ref[...] = mine_ref[...]


def split_kernel(start, mine_ref, theirs_ref, out_ref):
    for at in range(out_ref.shape[0]):
        for part in range(2):
            out_ref[at, 0, part] = mine_ref[part, start + at]
            out_ref[at, 1, part] = theirs_ref[part, at]


def join_kernel(start, stop, *refs):
    out_ref = refs[-1]
    for slot, from_ref in enumerate(refs[:-1]):
        out_ref[slot] = from_ref[start:stop]


def pack_kernel(sigma_ref, green_ref, out_ref, own_ref):
    core = place()[4]
    out_ref[0:2] = sigma_ref[...]
    out_ref[2:4] = green_ref[:, :, pl.ds(pl.multiple_of((1 - core) * TB, TB), TB)]
    own_ref[...] = green_ref[:, :, pl.ds(pl.multiple_of(core * TB, TB), TB)]


def prepare_kernel(packed_ref, own_ref, swapped_ref, even_ref, odd_ref, both_ref, state_ref, base_ref, link_ref):
    core = place()[4]
    first = core == 0
    own = own_ref[...]
    even_ref[...] = jnp.where(first, packed_ref[0:2], swapped_ref[0:2])
    odd_ref[...] = jnp.where(first, swapped_ref[0:2], packed_ref[0:2])
    state_ref[0] = jnp.where(first, own, swapped_ref[2:4])
    state_ref[1] = jnp.where(first, swapped_ref[2:4], own)
    real_part, imag_part = complex_dot(odd_ref[0], odd_ref[1], even_ref[0], even_ref[1])
    both_ref[0] = real_part.astype(BF16)
    both_ref[1] = imag_part.astype(BF16)
    set_base(odd_ref, state_ref, base_ref)
    for half in range(CHUNKS):
        put_link(link_ref.at[half], base_ref, half)


def put_link(link_ref, base_ref, half):
    columns = slice(half * WIDE, (half + 1) * WIDE)
    link_ref[:, :WIDE] = base_ref[0, :, columns].astype(BF16)
    link_ref[:, WIDE:] = base_ref[1, :, columns].astype(BF16)


def set_base(odd_ref, state_ref, base_ref):
    real_part, imag_part = complex_dot(odd_ref[0], odd_ref[1], state_ref[0, 0], state_ref[0, 1])
    base_ref[0] = real_part + state_ref[1, 0].astype(F32)
    base_ref[1] = imag_part + state_ref[1, 1].astype(F32)


def turned(left, right):
    return lax.dot_general(left, right, (((0,), (0,)), ((), ())), preferred_element_type=F32)


def put_history(tick, side, real_ref, imag_ref, past_ref, out_ref):
    rows = slice(tick * TB, (tick + HW) * TB)
    at = pl.ds(pl.multiple_of(side * TB, TB), TB)

    @pl.loop(0, 2)
    def _(part):
        by_imag = turned(imag_ref[...], past_ref[1 - part, rows, at])
        by_imag = jnp.where(part == 0, -by_imag, by_imag)
        out_ref[part] = (turned(real_ref[...], past_ref[part, rows, at]) + by_imag).astype(BF16)


def keep_kernel(tick, real_ref, imag_ref, past_ref, out_ref):
    put_history(tick, place()[4], real_ref, imag_ref, past_ref, out_ref)


def history_kernel(tick, stacked, *refs):
    sigma_refs = refs[:4]
    past_ref, give_ref, real_ref, imag_ref = refs[4:]
    x, high, y, _, core = place()
    upright = core == 0
    for outer in range(4):
        for inner in range(4):
            x_at = (x + jnp.where(upright, OFFSETS[outer], OFFSETS[inner]) + 4) % 4
            y_at = (y + jnp.where(upright, OFFSETS[inner], OFFSETS[outer]) + 4) % 4
            for deep in range(2):
                at = pl.ds(pl.multiple_of((x_at * 8 + (high ^ deep) * 4 + y_at) * 32, 32), 32)
                real_ref[at, :] = sigma_refs[outer][inner, stacked, deep, 0]
                imag_ref[at, :] = sigma_refs[outer][inner, stacked, deep, 1]

    put_history(tick, 1 - core, real_ref, imag_ref, past_ref, give_ref)


def link_kernel(half, early, both_ref, carry_ref, base_ref, out_ref):
    chip = place()[3]

    @pl.when(chip == 0)
    def _():
        put_link(out_ref, base_ref, half)

    @pl.when(chip > 0)
    def _():
        carry = carry_ref[half] if early else carry_ref[...]
        columns = slice(half * WIDE, (half + 1) * WIDE)
        by_real = dot(both_ref[0], carry)
        by_imag = dot(both_ref[1], carry)
        out_ref[:, :WIDE] = (by_real[:, :WIDE] - by_imag[:, WIDE:] + base_ref[0, :, columns]).astype(BF16)
        out_ref[:, WIDE:] = (by_real[:, WIDE:] + by_imag[:, :WIDE] + base_ref[1, :, columns]).astype(BF16)


def update_kernel(step, ticks, n_carry, *refs):
    refs = list(refs)
    last = step == 6
    even_ref, odd_ref, state_ref, base_ref = refs[:4]
    carry_refs = refs[4 : 4 + n_carry]
    refs = refs[4 + n_carry :]
    pasts = [(refs.pop(0), refs.pop(0)) for _ in ticks]
    out_ref, other_ref, past_ref = refs
    _, _, _, chip, core = place()
    valid = (chip <= step) & (chip >= step - (TICKS - 1))

    def copy_past(keep_ref, swap_ref):
        first = core == 0
        past_ref[0] = jnp.where(first, keep_ref[...], swap_ref[...])
        past_ref[1] = jnp.where(first, swap_ref[...], keep_ref[...])

    @pl.when(valid)
    def _():
        for tick, (keep_ref, swap_ref) in zip(ticks, pasts):
            pl.when(chip == step - tick)(functools.partial(copy_past, keep_ref, swap_ref))
        state = [[state_ref[block, part].astype(F32) for part in range(2)] for block in range(2)]
        even_carry = [jnp.zeros((TB, TB), F32)] * 2
        odd_carry = state[0]
        if n_carry:
            inside = chip > 0
            halves = [carry_refs[0][half] for half in range(CHUNKS)] if step == 1 else [ref[...] for ref in carry_refs]
            carry = [
                jnp.concatenate([half[:, part * WIDE : (part + 1) * WIDE] for half in halves], axis=1)
                for part in range(2)
            ]
            carry = [jnp.where(inside, part, jnp.zeros((TB, TB), BF16)) for part in carry]
            even_carry = [part.astype(F32) for part in carry]
            moved = complex_dot(even_ref[0], even_ref[1], carry[0], carry[1])
            odd_carry = [moved[part] + state[0][part] for part in range(2)]
        carries = (even_carry, odd_carry)
        new_ref = past_ref if last else out_ref
        for block in range(2):
            past = [past_ref[block, part].astype(F32) for part in range(2)]
            new_real = state[block][0] + TIME_STEP * (past[1] + carries[block][1])
            new_imag = state[block][1] - TIME_STEP * (past[0] + carries[block][0])
            new_ref[block, 0] = new_real.astype(BF16)
            new_ref[block, 1] = new_imag.astype(BF16)
        if not last:
            set_base(odd_ref, out_ref, other_ref)

    @pl.when(jnp.logical_not(valid))
    def _():
        if last:
            past_ref[...] = state_ref[...]
        else:
            out_ref[...] = state_ref[...]
            other_ref[...] = base_ref[...]

    if last:
        first = core == 0
        out_ref[...] = jnp.where(first, past_ref[0], past_ref[1])
        other_ref[...] = jnp.where(first, past_ref[1], past_ref[0])


def mirror_kernel(resident_ref, keep_ref, swap_ref, out_ref):
    core = place()[4]

    def across(left, right):
        return lax.dot_general(left, right, (((1,), (1,)), ((), ())), preferred_element_type=F32)

    real_part = jnp.zeros((TB, TB), F32)
    imag_part = jnp.zeros((TB, TB), F32)
    for green_ref, side in ((keep_ref, core), (swap_ref, 1 - core)):
        at = pl.ds(pl.multiple_of(side * TB, TB), TB)
        held_real, held_imag = resident_ref[0, :, at], resident_ref[1, :, at]
        real_part += across(held_real, green_ref[0]) + across(held_imag, green_ref[1])
        imag_part += across(held_imag, green_ref[0]) - across(held_real, green_ref[1])
    out_ref[0] = real_part.astype(BF16)
    out_ref[1] = imag_part.astype(BF16)


def steps(green, step_sigma, hist_sigma, green_hist, resident):
    core = lax.axis_index("col") % 2
    square = (2, TB, TB)
    unit = 8 * TB**3
    pair = (shape(square, BF16), shape(square, BF16))
    state_shape = (shape((2, *square), BF16), shape(square, F32))

    mine = jnp.swapaxes(hist_sigma, 2, 3)
    theirs = [send(mine[:, start:stop], other_high) for start, stop in BATCHES]
    loaded = call(load_kernel, shape(mine.shape, BF16), [], TB, 1 << 18, mine)

    packed, own_green = call(
        pack_kernel, (shape((4, TB, TB), BF16), shape(square, BF16)), [], TB, 1 << 20, step_sigma, green
    )
    swapped = send(packed, other_core)
    partner_resident = send(resident, other_branch)
    even, odd, both, state, base, link = call(
        prepare_kernel, (shape(square, BF16), *pair, *state_shape, shape((CHUNKS, TB, 2 * WIDE), BF16)),
        [], 2 * unit, 4 << 20, packed, own_green, swapped,
    )
    carries = [send(link, next_chip(0))]

    pasts = []
    for batch, (start, stop) in enumerate(BATCHES):
        own = call(
            functools.partial(split_kernel, start),
            shape((stop - start, 2, 2, 32, TB), BF16), [], TB, 1 << 19, loaded, theirs[batch],
        )
        near = [own] + [send(own, early_axis(by)) for by in SHIFTS]
        for first, end in PARTS[batch]:
            block = call(
                functools.partial(join_kernel, first - start, end - start),
                shape((4, end - first, 2, 2, 32, TB), BF16), [], TB, 1 << 20, *near,
            )
            far = [send(block, late_axis(by)) for by in SHIFTS]
            for tick in range(first, end):
                table = shape((HW * TB, TB), BF16)
                give, real, imag = call(
                    functools.partial(history_kernel, tick, tick - first),
                    (shape(square, BF16), table, table), [], 4 * unit, 4 << 20, block, *far, green_hist,
                )
                traded = send(give, other_core)
                keep = call(
                    functools.partial(keep_kernel, tick),
                    shape(square, BF16), [], 4 * unit, 3 << 20, real, imag, green_hist,
                )
                pasts.append((keep, traded))

    for step in range(7):
        new_carries = carries
        if 0 < step < 6:
            new_carries = []
            for half in range(CHUNKS):
                early = step == 1
                link = call(
                    functools.partial(link_kernel, half, early),
                    shape((TB, 2 * WIDE), BF16), [], unit, 1 << 19, both, carries[0 if early else half], base,
                )
                new_carries.append(send(link, next_chip(step)))
        ticks = [step - chip for chip in range(4) if 0 <= step - chip < TICKS]
        used = carries if step else []
        args = [even, odd, state, base, *used]
        for tick in ticks:
            args.extend(pasts[tick])
        state, base = call(
            functools.partial(update_kernel, step, ticks, len(used)),
            pair if step == 6 else state_shape, [pltpu.VMEM((2, *square), BF16)], 2 * unit, 4 << 20, *args,
        )
        carries = new_carries

    keep, give = state, base
    got = send(give, other_core)
    mirrored = call(mirror_kernel, shape(square, BF16), [], 2 * unit, 2 << 20, partner_resident, keep, got)
    mirror_out = send(mirrored, other_branch)
    green_out = jnp.where(core == 0, jnp.concatenate([keep, got], axis=2), jnp.concatenate([got, keep], axis=2))
    return green_out, mirror_out


def solution(mesh):
    placed = (
        P(None, "col", "row"),
        P(None, "col", None),
        P(None, None, "col", "row"),
        P(None, None, "row"),
        P(None, "col", "row"),
    )
    return jax.shard_map(
        steps,
        mesh=mesh,
        in_specs=placed,
        out_specs=(P(None, "col", "row"), P(None, "col", "row")),
        check_vma=False,
    )
```

```python
import functools

import jax
import jax.numpy as jnp
from jax import lax
from jax.experimental import pallas as pl
from jax.experimental.pallas import tpu as pltpu
from jax.sharding import PartitionSpec as P


TB = 256
CHUNKS = 2
SHIFTS = (1, -1, 2)
OFFSETS = (0, -1, 1, 2)
BATCHES = ((0, 2), (2, 4))
PARTS = (((0, 1), (1, 2)), ((2, 4),))
WIDE = TB // CHUNKS
HW = 4
TICKS = 4
TIME_STEP = 0.2
BOTH = ("row", "col")
F32 = jnp.float32
BF16 = jnp.bfloat16


VMEM = pl.BlockSpec(memory_space=pltpu.VMEM)


def pairs_of(move):
    pairs = []
    for row in range(32):
        for col in range(8):
            there = move(row // 8, (row // 4) % 2, row % 4, col // 2, col % 2)
            x, high, y, chip, core = there
            pairs.append((row * 8 + col, (x * 8 + high * 4 + y) * 8 + chip * 2 + core))
    return pairs


def send(value, move):
    return lax.ppermute(value, BOTH, pairs_of(move))


def early_axis(by):
    def move(x, high, y, chip, core):
        return (x, high, (y + by) % 4, chip, core) if core == 0 else ((x + by) % 4, high, y, chip, core)

    return move


def late_axis(by):
    def move(x, high, y, chip, core):
        return ((x + by) % 4, high, y, chip, core) if core == 0 else (x, high, (y + by) % 4, chip, core)

    return move


def other_high(x, high, y, chip, core):
    return x, high ^ 1, y, chip, core


def other_core(x, high, y, chip, core):
    return x, high, y, chip, core ^ 1


def other_branch(x, high, y, chip, core):
    return x ^ 2, high, y, chip, core


def next_chip(step):
    first = max(step - (TICKS - 1), 0)
    last = min(step, 2) + 1

    def move(x, high, y, chip, core):
        if first <= chip < last:
            return x, high, y, chip + 1, core
        if chip == last:
            return x, high, y, first, core
        return x, high, y, chip, core ^ 1

    return move


def call(kernel, outs, scratch, flops, moved, *args):
    specs = [VMEM] * len(args)
    return pl.pallas_call(
        kernel,
        out_shape=outs,
        in_specs=specs,
        out_specs=jax.tree.map(lambda _: VMEM, outs),
        scratch_shapes=scratch,
        compiler_params=pltpu.CompilerParams(vmem_limit_bytes=24 << 20),
        cost_estimate=pl.CostEstimate(flops=flops, bytes_accessed=moved, transcendentals=0),
    )(*args)


def dot(left, right):
    return jnp.dot(left, right, preferred_element_type=F32)


def complex_dot(left_real, left_imag, right_real, right_imag):
    real_part = dot(left_real, right_real) - dot(left_imag, right_imag)
    imag_part = dot(left_real, right_imag) + dot(left_imag, right_real)
    return real_part, imag_part


def shape(dims, dtype):
    return jax.ShapeDtypeStruct(dims, dtype)


def place():
    row = lax.axis_index("row")
    col = lax.axis_index("col")
    return row // 8, (row // 4) % 2, row % 4, col // 2, col % 2


def load_kernel(mine_ref, out_ref):
    out_ref[...] = mine_ref[...]


def split_kernel(start, mine_ref, theirs_ref, out_ref):
    for at in range(out_ref.shape[0]):
        for part in range(2):
            out_ref[at, 0, part] = mine_ref[part, start + at]
            out_ref[at, 1, part] = theirs_ref[part, at]


def join_kernel(start, stop, *refs):
    out_ref = refs[-1]
    for slot, from_ref in enumerate(refs[:-1]):
        out_ref[slot] = from_ref[start:stop]


def pack_kernel(sigma_ref, green_ref, out_ref, own_ref):
    core = place()[4]
    out_ref[0:2] = sigma_ref[...]
    out_ref[2:4] = green_ref[:, :, pl.ds(pl.multiple_of((1 - core) * TB, TB), TB)]
    own_ref[...] = green_ref[:, :, pl.ds(pl.multiple_of(core * TB, TB), TB)]


def prepare_kernel(packed_ref, own_ref, swapped_ref, even_ref, odd_ref, both_ref, state_ref, base_ref, link_ref):
    core = place()[4]
    first = core == 0
    own = own_ref[...]
    even_ref[...] = jnp.where(first, packed_ref[0:2], swapped_ref[0:2])
    odd_ref[...] = jnp.where(first, swapped_ref[0:2], packed_ref[0:2])
    state_ref[0] = jnp.where(first, own, swapped_ref[2:4])
    state_ref[1] = jnp.where(first, swapped_ref[2:4], own)
    real_part, imag_part = complex_dot(odd_ref[0], odd_ref[1], even_ref[0], even_ref[1])
    both_ref[0] = real_part.astype(BF16)
    both_ref[1] = imag_part.astype(BF16)
    set_base(odd_ref, state_ref, base_ref)
    for half in range(CHUNKS):
        put_link(link_ref.at[half], base_ref, half)


def put_link(link_ref, base_ref, half):
    columns = slice(half * WIDE, (half + 1) * WIDE)
    link_ref[:, :WIDE] = base_ref[0, :, columns].astype(BF16)
    link_ref[:, WIDE:] = base_ref[1, :, columns].astype(BF16)


def set_base(odd_ref, state_ref, base_ref):
    real_part, imag_part = complex_dot(odd_ref[0], odd_ref[1], state_ref[0, 0], state_ref[0, 1])
    base_ref[0] = real_part + state_ref[1, 0].astype(F32)
    base_ref[1] = imag_part + state_ref[1, 1].astype(F32)


def turned(left, right):
    return lax.dot_general(left, right, (((0,), (0,)), ((), ())), preferred_element_type=F32)


def put_history(tick, side, unroll, real_ref, imag_ref, past_ref, out_ref):
    rows = slice(tick * TB, (tick + HW) * TB)
    at = pl.ds(pl.multiple_of(side * TB, TB), TB)

    @pl.loop(0, 2, unroll=unroll)
    def _(part):
        by_imag = turned(imag_ref[...], past_ref[1 - part, rows, at])
        by_imag = jnp.where(part == 0, -by_imag, by_imag)
        out_ref[part] = (turned(real_ref[...], past_ref[part, rows, at]) + by_imag).astype(BF16)


def keep_kernel(tick, real_ref, imag_ref, past_ref, out_ref):
    put_history(tick, place()[4], False, real_ref, imag_ref, past_ref, out_ref)


def history_kernel(tick, stacked, *refs):
    sigma_refs = refs[:4]
    past_ref, give_ref, real_ref, imag_ref = refs[4:]
    x, high, y, _, core = place()
    upright = core == 0
    for outer in range(4):
        for inner in range(4):
            x_at = (x + jnp.where(upright, OFFSETS[outer], OFFSETS[inner]) + 4) % 4
            y_at = (y + jnp.where(upright, OFFSETS[inner], OFFSETS[outer]) + 4) % 4
            for deep in range(2):
                at = pl.ds(pl.multiple_of((x_at * 8 + (high ^ deep) * 4 + y_at) * 32, 32), 32)
                real_ref[at, :] = sigma_refs[outer][inner, stacked, deep, 0]
                imag_ref[at, :] = sigma_refs[outer][inner, stacked, deep, 1]

    put_history(tick, 1 - core, True, real_ref, imag_ref, past_ref, give_ref)


def link_kernel(half, early, both_ref, carry_ref, base_ref, out_ref):
    chip = place()[3]

    @pl.when(chip == 0)
    def _():
        put_link(out_ref, base_ref, half)

    @pl.when(chip > 0)
    def _():
        carry = carry_ref[half] if early else carry_ref[...]
        columns = slice(half * WIDE, (half + 1) * WIDE)
        by_real = dot(both_ref[0], carry)
        by_imag = dot(both_ref[1], carry)
        out_ref[:, :WIDE] = (by_real[:, :WIDE] - by_imag[:, WIDE:] + base_ref[0, :, columns]).astype(BF16)
        out_ref[:, WIDE:] = (by_real[:, WIDE:] + by_imag[:, :WIDE] + base_ref[1, :, columns]).astype(BF16)


def update_kernel(step, ticks, n_carry, *refs):
    refs = list(refs)
    last = step == 6
    even_ref, odd_ref, state_ref, base_ref = refs[:4]
    carry_refs = refs[4 : 4 + n_carry]
    refs = refs[4 + n_carry :]
    pasts = [(refs.pop(0), refs.pop(0)) for _ in ticks]
    out_ref, other_ref, past_ref = refs
    _, _, _, chip, core = place()
    valid = (chip <= step) & (chip >= step - (TICKS - 1))

    def copy_past(keep_ref, swap_ref):
        first = core == 0
        past_ref[0] = jnp.where(first, keep_ref[...], swap_ref[...])
        past_ref[1] = jnp.where(first, swap_ref[...], keep_ref[...])

    @pl.when(valid)
    def _():
        for tick, (keep_ref, swap_ref) in zip(ticks, pasts):
            pl.when(chip == step - tick)(functools.partial(copy_past, keep_ref, swap_ref))
        state = [[state_ref[block, part].astype(F32) for part in range(2)] for block in range(2)]
        even_carry = [jnp.zeros((TB, TB), F32)] * 2
        odd_carry = state[0]
        if n_carry:
            inside = chip > 0
            halves = [carry_refs[0][half] for half in range(CHUNKS)] if step == 1 else [ref[...] for ref in carry_refs]
            carry = [
                jnp.concatenate([half[:, part * WIDE : (part + 1) * WIDE] for half in halves], axis=1)
                for part in range(2)
            ]
            carry = [jnp.where(inside, part, jnp.zeros((TB, TB), BF16)) for part in carry]
            even_carry = [part.astype(F32) for part in carry]
            moved = complex_dot(even_ref[0], even_ref[1], carry[0], carry[1])
            odd_carry = [moved[part] + state[0][part] for part in range(2)]
        carries = (even_carry, odd_carry)
        new_ref = past_ref if last else out_ref
        for block in range(2):
            past = [past_ref[block, part].astype(F32) for part in range(2)]
            new_real = state[block][0] + TIME_STEP * (past[1] + carries[block][1])
            new_imag = state[block][1] - TIME_STEP * (past[0] + carries[block][0])
            new_ref[block, 0] = new_real.astype(BF16)
            new_ref[block, 1] = new_imag.astype(BF16)
        if not last:
            set_base(odd_ref, out_ref, other_ref)

    @pl.when(jnp.logical_not(valid))
    def _():
        if last:
            past_ref[...] = state_ref[...]
        else:
            out_ref[...] = state_ref[...]
            other_ref[...] = base_ref[...]

    if last:
        first = core == 0
        out_ref[...] = jnp.where(first, past_ref[0], past_ref[1])
        other_ref[...] = jnp.where(first, past_ref[1], past_ref[0])


def mirror_kernel(resident_ref, keep_ref, swap_ref, out_ref):
    core = place()[4]

    def across(left, right):
        return lax.dot_general(left, right, (((1,), (1,)), ((), ())), preferred_element_type=F32)

    real_part = jnp.zeros((TB, TB), F32)
    imag_part = jnp.zeros((TB, TB), F32)
    for green_ref, side in ((keep_ref, core), (swap_ref, 1 - core)):
        at = pl.ds(pl.multiple_of(side * TB, TB), TB)
        held_real, held_imag = resident_ref[0, :, at], resident_ref[1, :, at]
        real_part += across(held_real, green_ref[0]) + across(held_imag, green_ref[1])
        imag_part += across(held_imag, green_ref[0]) - across(held_real, green_ref[1])
    out_ref[0] = real_part.astype(BF16)
    out_ref[1] = imag_part.astype(BF16)


def steps(green, step_sigma, hist_sigma, green_hist, resident):
    core = lax.axis_index("col") % 2
    square = (2, TB, TB)
    unit = 8 * TB**3
    pair = (shape(square, BF16), shape(square, BF16))
    state_shape = (shape((2, *square), BF16), shape(square, F32))

    mine = jnp.swapaxes(hist_sigma, 2, 3)
    theirs = [send(mine[:, start:stop], other_high) for start, stop in BATCHES]
    loaded = call(load_kernel, shape(mine.shape, BF16), [], TB, 1 << 18, mine)

    packed, own_green = call(
        pack_kernel, (shape((4, TB, TB), BF16), shape(square, BF16)), [], TB, 1 << 20, step_sigma, green
    )
    swapped = send(packed, other_core)
    partner_resident = send(resident, other_branch)
    even, odd, both, state, base, link = call(
        prepare_kernel, (shape(square, BF16), *pair, *state_shape, shape((CHUNKS, TB, 2 * WIDE), BF16)),
        [], 2 * unit, 4 << 20, packed, own_green, swapped,
    )
    carries = [send(link, next_chip(0))]

    pasts = []
    for batch, (start, stop) in enumerate(BATCHES):
        own = call(
            functools.partial(split_kernel, start),
            shape((stop - start, 2, 2, 32, TB), BF16), [], TB, 1 << 19, loaded, theirs[batch],
        )
        near = [own] + [send(own, early_axis(by)) for by in SHIFTS]
        for first, end in PARTS[batch]:
            block = call(
                functools.partial(join_kernel, first - start, end - start),
                shape((4, end - first, 2, 2, 32, TB), BF16), [], TB, 1 << 20, *near,
            )
            far = [send(block, late_axis(by)) for by in SHIFTS]
            for tick in range(first, end):
                table = shape((HW * TB, TB), BF16)
                give, real, imag = call(
                    functools.partial(history_kernel, tick, tick - first),
                    (shape(square, BF16), table, table), [], 4 * unit, 4 << 20, block, *far, green_hist,
                )
                traded = send(give, other_core)
                keep = call(
                    functools.partial(keep_kernel, tick),
                    shape(square, BF16), [], 4 * unit, 3 << 20, real, imag, green_hist,
                )
                pasts.append((keep, traded))

    for step in range(7):
        new_carries = carries
        if 0 < step < 6:
            new_carries = []
            for half in range(CHUNKS):
                early = step == 1
                link = call(
                    functools.partial(link_kernel, half, early),
                    shape((TB, 2 * WIDE), BF16), [], unit, 1 << 19, both, carries[0 if early else half], base,
                )
                new_carries.append(send(link, next_chip(step)))
        ticks = [step - chip for chip in range(4) if 0 <= step - chip < TICKS]
        used = carries if step else []
        args = [even, odd, state, base, *used]
        for tick in ticks:
            args.extend(pasts[tick])
        state, base = call(
            functools.partial(update_kernel, step, ticks, len(used)),
            pair if step == 6 else state_shape, [pltpu.VMEM((2, *square), BF16)], 2 * unit, 4 << 20, *args,
        )
        carries = new_carries

    keep, give = state, base
    got = send(give, other_core)
    mirrored = call(mirror_kernel, shape(square, BF16), [], 2 * unit, 2 << 20, partner_resident, keep, got)
    mirror_out = send(mirrored, other_branch)
    green_out = jnp.where(core == 0, jnp.concatenate([keep, got], axis=2), jnp.concatenate([got, keep], axis=2))
    return green_out, mirror_out


def solution(mesh):
    placed = (
        P(None, "col", "row"),
        P(None, "col", None),
        P(None, None, "col", "row"),
        P(None, None, "row"),
        P(None, "col", "row"),
    )
    return jax.shard_map(
        steps,
        mesh=mesh,
        in_specs=placed,
        out_specs=(P(None, "col", "row"), P(None, "col", "row")),
        check_vma=False,
    )
```
